32 devices in a mesh: dp: 2 (over x), seq: 16 (over z, y, core).
Axes of the slice: x: 2, y: 2, z: 4, core: 2. Of those that a mesh axis runs over, the one named last changes fastest.
Arguments:
- tokens: bfloat16 [2, 2048, 1536], P('dp', 'seq'), may hold values from -6 to 6
- query_weight: bfloat16 [1536, 1024], P('seq'), may hold values from -0.15564466 to 0.15564466
- key_weight: bfloat16 [1536, 128], P('seq'), may hold values from -7.6546554 to 7.6546554
- value_weight: bfloat16 [1536, 128], P('seq'), may hold values from -0.15625 to 0.15625
- output_weight: bfloat16 [1536, 1024], P('seq'), may hold values from -0.1875 to 0.1875
- row_weight: bfloat16 [1536, 128], replicated, may hold values from -0.15625 to 0.15625
- col_weight: bfloat16 [1536, 128], replicated, may hold values from -0.15625 to 0.15625
- pair_cotangent: bfloat16 [2, 128, 128, 128], P('dp', 'seq'), may hold values from -0.046875 to 0.046875
Outputs:
- pair: bfloat16 [2, 128, 128, 128], P('dp', 'seq')
- grad_row_weight: bfloat16 [1536, 128], replicated
- grad_col_weight: bfloat16 [1536, 128], replicated
The draws below stay inside these ranges and needn't reach their ends.
All inputs are finite; a program needn't handle non-finite values.
Results may differ from the reference program's by a relative error of at most 0.025.
The reference program's roundings to bfloat16 on the way (of `normed`, `rounded`, `attended` and `bin_feat`) count: a program that leaves them out, or rounds other values in their place, can miss the bound.
Values may be sent and summed in bfloat16 or wider, within the bound.
A program may use at most 64 MiB of HBM per device.

```python
import math
import jax
import jax.numpy as jnp
from jax import lax

D = 1536
HEADS = 8
HD = 128
PAIR_C = 128
POOL = 16
SEQ_LEN = 2048
BINS = 128
SAMPLES = 2


def shared_query(key):
    base = jax.random.truncated_normal(jax.random.fold_in(key, 11), -6.0, 6.0, (D, HEADS * HD), jnp.float32)
    return base / math.sqrt(D)


def draw_query_weight(key, part):
    return shared_query(key).astype(jnp.bfloat16)


def draw_key_weight(key, part):
    noise = jax.random.truncated_normal(jax.random.fold_in(key, 12), -6.0, 6.0, (D, HD), jnp.float32) / math.sqrt(D)
    return noise.astype(jnp.bfloat16)


def draw_tokens(key, part):
    base = jax.random.truncated_normal(jax.random.fold_in(key, 21), -6.0, 6.0, (SAMPLES, SEQ_LEN, D), jnp.float32)
    return base.astype(jnp.bfloat16)


def with_spikes(entries, key, source, target, parts, factor):
    def block_of(dim):
        return (jnp.arange(entries.shape[dim]) // (entries.shape[dim] // parts)).reshape((-1,) + (1,) * (entries.ndim - 1 - dim))

    near = jax.random.permutation(key, parts)[block_of(target)]
    second = (block_of(target) + parts // 2) % parts
    return jnp.where((block_of(source) == near) | (block_of(source) == second), factor * entries, entries)


def block_levels(own_key, dims, pieces, smallest, largest):
    level, own = 1.0, jax.random.fold_in(own_key, 6)
    for dim, shards_of in pieces:
        heights = jnp.exp(jax.random.uniform(jax.random.fold_in(own, dim), (shards_of,), jnp.float32, smallest / len(pieces), largest / len(pieces)))
        level = level * jnp.repeat(heights, dims[dim] // shards_of).reshape([-1 if axis == dim else 1 for axis in range(len(dims))])
    return level


def centred(stream_key, shape, deviation, limit, shards=(), dtype=jnp.bfloat16):
    gain = block_levels(stream_key, shape, shards, -0.22, 0.18) if shards else 1.0
    array = jax.random.normal(stream_key, shape, jnp.float32) * deviation * gain
    return jnp.minimum(jnp.maximum(array, -limit), limit).astype(dtype)


def heavy_noise(rng, dims, scale, most, cuts, heavy, dtype=jnp.bfloat16):
    entries = scale * jax.random.normal(rng, dims, jnp.float32)
    if cuts:
        entries = entries * block_levels(rng, dims, cuts, -0.22, 0.18)
    return jnp.clip(with_spikes(entries, jax.random.fold_in(rng, 3), *heavy), -most, most).astype(dtype)


def setup_inputs(seed: int = 0) -> dict:
    seeds = jax.random.split(jax.random.key(seed), 9)
    tokens = draw_tokens(jax.random.fold_in(seeds[8], 71), 0)
    query_weight = draw_query_weight(jax.random.fold_in(seeds[8], 71), 0)
    key_weight = draw_key_weight(jax.random.fold_in(seeds[8], 71), 0)
    value_weight = centred(seeds[3], (D, HD), D ** -0.5, 0.15625, ((0, 16),))
    output_weight = centred(seeds[4], (D, HEADS * HD), (HEADS * HD) ** -0.5, 0.1875, ((0, 16),))
    row_weight = centred(seeds[5], (D, PAIR_C), D ** -0.5, 0.15625)
    col_weight = centred(seeds[6], (D, PAIR_C), D ** -0.5, 0.15625)
    pair_cotangent = heavy_noise(seeds[7], (SAMPLES, BINS, BINS, PAIR_C), (1.0 / BINS), 0.046875, ((0, 2), (1, 16)), (1, 2, 16, 2.0))
    return dict(tokens=tokens, query_weight=query_weight, key_weight=key_weight, value_weight=value_weight, output_weight=output_weight, row_weight=row_weight, col_weight=col_weight, pair_cotangent=pair_cotangent)


def rms_rows(values):
    return values * lax.rsqrt(lax.optimization_barrier(jnp.mean(values * values, axis=-1, keepdims=True)) + 1e-06)

def one_sample(tokens, cotangent, query_weight, key_weight, value_weight, output_weight, row_weight, col_weight):
    normed = rms_rows(tokens.astype(jnp.float32)).astype(jnp.bfloat16)
    queries = jnp.dot(normed, query_weight, preferred_element_type=jnp.float32).astype(jnp.bfloat16)
    keys = jnp.dot(normed, key_weight, preferred_element_type=jnp.float32).astype(jnp.bfloat16)
    values = jnp.dot(normed, value_weight, preferred_element_type=jnp.float32).astype(jnp.bfloat16)
    keys_wide = keys.astype(jnp.float32)
    values_wide = values.astype(jnp.float32)
    rows_all = SEQ_LEN * HEADS
    block = math.gcd(1024, rows_all)
    query_rows = queries.reshape(rows_all // block, block, HD).astype(jnp.float32)
    scale = 1.0 / math.sqrt(HD)

    def attend(query_block):
        scores = jnp.dot(query_block, keys_wide.T) * scale
        weights = jnp.exp(scores - lax.optimization_barrier(jnp.max(scores, axis=1, keepdims=True)))
        total = lax.optimization_barrier(jnp.sum(weights, axis=1, keepdims=True))
        rounded = weights.astype(jnp.bfloat16).astype(jnp.float32)
        return (jnp.dot(rounded, values_wide) / total).astype(jnp.bfloat16)
    attended = lax.map(attend, query_rows).reshape(SEQ_LEN, HEADS * HD)
    update = jnp.dot(attended.astype(jnp.float32), output_weight.astype(jnp.float32).T)
    pooled = lax.optimization_barrier(jnp.mean(update.reshape(BINS, POOL, D), axis=1))
    bin_feat = rms_rows(pooled).astype(jnp.bfloat16)
    row_proj = jnp.dot(bin_feat, row_weight, preferred_element_type=jnp.float32).astype(jnp.bfloat16)
    col_proj = jnp.dot(bin_feat, col_weight, preferred_element_type=jnp.float32).astype(jnp.bfloat16)
    row_wide = row_proj.astype(jnp.float32)
    col_wide = col_proj.astype(jnp.float32)
    pair = (row_wide[:, None, :] * col_wide[None, :, :]).astype(jnp.bfloat16)
    cot_wide = cotangent.astype(jnp.float32)
    row_grad = jnp.einsum('ijc,jc->ic', cot_wide, col_wide).astype(jnp.bfloat16)
    col_grad = jnp.einsum('ijc,ic->jc', cot_wide, row_wide).astype(jnp.bfloat16)
    feat_wide = bin_feat.astype(jnp.float32)
    grad_row = jnp.dot(feat_wide.T, row_grad.astype(jnp.float32))
    grad_col = jnp.dot(feat_wide.T, col_grad.astype(jnp.float32))
    return (pair, grad_row, grad_col)

def reference(tokens, query_weight, key_weight, value_weight, output_weight, row_weight, col_weight, pair_cotangent):
    pairs = []
    grad_row = jnp.zeros((D, PAIR_C), jnp.float32)
    grad_col = jnp.zeros((D, PAIR_C), jnp.float32)
    for sample in range(SAMPLES):
        pair, g_row, g_col = one_sample(tokens[sample], pair_cotangent[sample], query_weight, key_weight, value_weight, output_weight, row_weight, col_weight)
        pairs.append(pair)
        grad_row = grad_row + g_row
        grad_col = grad_col + g_col
    return (jnp.stack(pairs, 0), grad_row.astype(jnp.bfloat16), grad_col.astype(jnp.bfloat16))
```

```python
import functools
import math

import jax
import jax.numpy as jnp
from jax import lax
from jax.experimental import pallas as pl
from jax.experimental.pallas import tpu as pltpu
from jax.sharding import PartitionSpec as P

POOL = 16
LINE = 4
F32 = jnp.float32
BF16 = jnp.bfloat16
MESH = pl.DeviceIdType.MESH
LAST = (((1,), (1,)), ((), ()))


def merge_rows(block, rows):
    if block.shape[1] % 16 == 0:
        return block.reshape(rows, block.shape[2])
    return block.astype(F32).reshape(rows, block.shape[2]).astype(block.dtype)


class Where:
    def __init__(self, n_dp, n_seq):
        self.n_dp, self.n_seq = n_dp, n_seq
        self.mid = n_seq // (LINE * 2)
        self.dp, self.me = lax.axis_index("dp"), lax.axis_index("seq")
        self.core = self.me % 2
        self.y = (self.me // 2) % self.mid
        self.z = self.me // (2 * self.mid)

    def at(self, dz, dy, flip):
        z = (self.z + dz) % LINE
        y = (self.y + dy) % self.mid
        core = 1 - self.core if flip else self.core
        return (z * self.mid + y) * 2 + core

    def near(self):
        return (
            [self.at(dz, 0, False) for dz in range(1, LINE)]
            + [self.at(0, dy, False) for dy in range(1, self.mid)]
            + [self.at(0, 0, True)]
        )


class Gather:
    def __init__(self, where, slot, send_sem, recv_sem):
        self.w, self.slot = where, slot
        self.send_sem, self.recv_sem = send_sem, recv_sem
        self.sent = []

    def push(self, block, peer):
        ref = self.slot(block)
        copy = pltpu.make_async_remote_copy(
            src_ref=ref,
            dst_ref=ref,
            send_sem=self.send_sem.at[len(self.sent)],
            recv_sem=self.recv_sem.at[block],
            device_id=(self.w.dp, peer),
            device_id_type=MESH,
        )
        copy.start()
        self.sent.append(copy)

    def arrived(self, block):
        ref = self.slot(block)
        pltpu.make_async_remote_copy(
            src_ref=ref,
            dst_ref=ref,
            send_sem=self.send_sem.at[0],
            recv_sem=self.recv_sem.at[block],
            device_id=(self.w.dp, self.w.me),
            device_id_type=MESH,
        ).wait_recv()

    def start(self):
        w = self.w
        for dz in (1, LINE - 1, *range(2, LINE - 1)):
            self.push(w.me, w.at(dz, 0, False))
        self.spread(0)

    def spread(self, dz):
        w = self.w
        block = w.at(dz, 0, False)
        for dy in range(1, w.mid):
            self.push(block, w.at(0, dy, False))
        self.push(block, w.at(0, 0, True))

    def pass_on(self):
        w = self.w
        order = (1, LINE - 1, *range(2, LINE - 1))
        for dz in order:
            self.arrived(w.at(dz, 0, False))
            self.spread(dz)
        for dz in (0, *order):
            for dy in range(1, w.mid):
                self.arrived(w.at(dz, dy, False))
                self.push(w.at(dz, dy, False), w.at(0, 0, True))

    def complete(self):
        w = self.w
        for dz in (0, 1, LINE - 1, *range(2, LINE - 1)):
            for dy in range(w.mid):
                self.arrived(w.at(dz, dy, True))

    def drain(self):
        for copy in self.sent:
            copy.wait_send()


def copies_of(n_seq):
    mid = n_seq // (LINE * 2)
    return (LINE - 1) + LINE * (mid - 1) + LINE * mid


def kv_kernel(
    n_dp, n_seq, tok_ref, wk_ref, wv_ref, normed_ref, kv_ref, w_buf, w_send, w_recv, k_send, k_recv
):
    w = Where(n_dp, n_seq)
    barrier = pltpu.get_barrier_semaphore()
    near = w.near()
    for peer in near:
        pl.semaphore_signal(barrier, inc=1, device_id=(w.dp, peer), device_id_type=MESH)
    head = wk_ref.shape[1]
    w_buf[w.me, :, 0:head] = wk_ref[...]
    w_buf[w.me, :, head : 2 * head] = wv_ref[...]
    pl.semaphore_wait(barrier, len(near))
    weights = Gather(w, lambda s: w_buf.at[s], w_send, w_recv)
    weights.start()
    tok = tok_ref[...].astype(F32)
    normed = (tok * lax.rsqrt(jnp.mean(tok * tok, axis=1, keepdims=True) + 1e-06)).astype(BF16)
    normed_ref[...] = normed
    weights.pass_on()
    weights.complete()
    width = tok_ref.shape[1]
    full = merge_rows(w_buf[...], width)
    kv_ref[w.me] = jnp.dot(normed, full, preferred_element_type=F32).astype(BF16)
    blocks = Gather(w, lambda s: kv_ref.at[s], k_send, k_recv)
    blocks.start()
    blocks.pass_on()
    blocks.complete()
    weights.drain()
    blocks.drain()


def main_kernel(
    n_dp,
    n_seq,
    normed_ref,
    kv_ref,
    w_hbm,
    roww_ref,
    colw_ref,
    cot_ref,
    pair_ref,
    grow_ref,
    gcol_ref,
    wq_buf,
    wo_buf,
    att,
    feats,
    terms,
    parts,
    grads,
    turned,
    load_sem,
    f_send,
    f_recv,
    x_send,
    x_recv,
    s_send,
    r_send,
    r_recv,
    g_send,
    g_recv,
):
    w = Where(n_dp, n_seq)
    dp, me = w.dp, w.me
    every = n_dp * n_seq
    flat = dp * n_seq + me
    half = n_seq // 2
    heads_wide = wq_buf.shape[1]
    width = wq_buf.shape[0]
    load_q = pltpu.make_async_copy(w_hbm.at[:, pl.ds(0, heads_wide)], wq_buf, load_sem.at[0])
    load_o = pltpu.make_async_copy(
        w_hbm.at[:, pl.ds(heads_wide, heads_wide)], wo_buf, load_sem.at[1]
    )
    load_q.start()
    load_o.start()

    barrier = pltpu.get_barrier_semaphore()

    def greet(t, unused):
        peer = (flat + t) % every
        pl.semaphore_signal(
            barrier, inc=1, device_id=(peer // n_seq, peer % n_seq), device_id_type=MESH
        )
        return unused

    lax.fori_loop(1, every, greet, 0)

    head = kv_ref.shape[2] // 2
    rows = normed_ref.shape[0]
    length = n_seq * rows
    load_q.wait()
    queries = jnp.dot(normed_ref[...], wq_buf[...], preferred_element_type=F32).astype(BF16)
    keys = kv_ref[:, :, 0:head].reshape(length, head)
    values = kv_ref[:, :, head : 2 * head].reshape(length, head)
    factor = math.log2(math.e) / math.sqrt(head)
    for h in range(0, heads_wide // head, 2):
        both = jnp.concatenate(
            [queries[:, h * head : (h + 1) * head], queries[:, (h + 1) * head : (h + 2) * head]],
            axis=0,
        )
        scores = lax.dot_general(both, keys, LAST, preferred_element_type=F32)
        top = jnp.max(scores, axis=1, keepdims=True)
        weights = jnp.exp2((scores - top) * factor)
        total = jnp.sum(weights, axis=1, keepdims=True)
        out = jnp.dot(weights.astype(BF16), values, preferred_element_type=F32) / total
        out = out.astype(BF16)
        att[:, h * head : (h + 1) * head] = out[0:rows]
        att[:, (h + 1) * head : (h + 2) * head] = out[rows : 2 * rows]
    load_o.wait()
    update = lax.dot_general(att[...], wo_buf[...], LAST, preferred_element_type=F32)
    bins = rows // POOL
    pooled = jnp.mean(update.reshape(bins, POOL, width), axis=1)
    scale = lax.rsqrt(jnp.mean(pooled * pooled, axis=1, keepdims=True) + 1e-06)
    feat = (pooled * scale).astype(BF16)
    feats[dp, me] = feat
    pl.semaphore_wait(barrier, every - 1)

    own = Gather(w, lambda s: feats.at[dp, s], f_send, f_recv)
    own.start()
    row_proj = jnp.dot(feat, roww_ref[...], preferred_element_type=F32).astype(BF16)
    own.pass_on()

    def across(d, k):
        slot = 2 * k + w.core
        ref = feats.at[dp, slot]
        return pltpu.make_async_remote_copy(
            src_ref=ref,
            dst_ref=ref,
            send_sem=x_send.at[d, k],
            recv_sem=x_recv.at[dp, slot],
            device_id=((dp + d) % n_dp, me),
            device_id_type=MESH,
        )

    def beside(d, k, flip):
        slot = 2 * k + (1 - w.core if flip else w.core)
        other = (dp + d) % n_dp
        ref = feats.at[other, slot]
        return pltpu.make_async_remote_copy(
            src_ref=ref,
            dst_ref=ref,
            send_sem=s_send.at[d, k],
            recv_sem=x_recv.at[other, slot],
            device_id=(dp, w.at(0, 0, True)),
            device_id_type=MESH,
        )

    def each(count, act):
        def step(k, unused):
            act(k)
            return unused

        lax.fori_loop(0, count, step, 0)

    for d in range(1, n_dp):
        each(half, lambda k: across(d, k).start())
    own.complete()

    count = n_seq * bins
    mine = merge_rows(feats[dp], count)
    col_proj = jnp.dot(mine, colw_ref[...], preferred_element_type=F32).astype(BF16)
    row_wide = row_proj.astype(F32)
    col_wide = col_proj.astype(F32)
    sums = jnp.zeros(col_wide.shape, F32)
    for i in range(bins):
        sums = sums + cot_ref[i].astype(F32) * row_wide[i : i + 1, :]
    terms[...] = sums.reshape(terms.shape)

    def scatter(t):
        peer = (me + t) % n_seq
        return pltpu.make_async_remote_copy(
            src_ref=terms.at[peer],
            dst_ref=parts.at[me],
            send_sem=r_send.at[t],
            recv_sem=r_recv.at[me],
            device_id=(dp, peer),
            device_id_type=MESH,
        )

    def scattered(t):
        peer = (me + t) % n_seq
        return pltpu.make_async_remote_copy(
            src_ref=terms.at[me],
            dst_ref=parts.at[peer],
            send_sem=r_send.at[t],
            recv_sem=r_recv.at[peer],
            device_id=(dp, peer),
            device_id_type=MESH,
        )

    each(n_seq - 1, lambda k: scatter(k + 1).start())
    parts[me] = terms[me]
    row_list = []
    for i in range(bins):
        pair_ref[i] = (row_wide[i : i + 1, :] * col_wide).astype(BF16)
        row_list.append(jnp.sum(cot_ref[i].astype(F32) * col_wide, axis=0, keepdims=True))
    row_grad = jnp.concatenate(row_list, axis=0)
    each(n_seq - 1, lambda k: scattered(k + 1).wait_recv())
    col_grad = jnp.sum(parts[...], axis=0)
    grads[flat] = jnp.concatenate([row_grad, col_grad], axis=1).astype(BF16)

    def share(t):
        peer = (flat + t) % every
        return pltpu.make_async_remote_copy(
            src_ref=grads.at[flat],
            dst_ref=grads.at[flat],
            send_sem=g_send.at[t],
            recv_sem=g_recv.at[flat],
            device_id=(peer // n_seq, peer % n_seq),
            device_id_type=MESH,
        )

    def shared(t):
        peer = (flat + t) % every
        return pltpu.make_async_remote_copy(
            src_ref=grads.at[peer],
            dst_ref=grads.at[peer],
            send_sem=g_send.at[t],
            recv_sem=g_recv.at[peer],
            device_id=(dp, me),
            device_id_type=MESH,
        )

    each(every - 1, lambda k: share(k + 1).start())

    for d in range(1, n_dp):

        def relay(k):
            slot = 2 * k + w.core
            other = (dp + d) % n_dp
            ref = feats.at[other, slot]
            pltpu.make_async_remote_copy(
                src_ref=ref,
                dst_ref=ref,
                send_sem=s_send.at[d, k],
                recv_sem=x_recv.at[other, slot],
                device_id=(dp, me),
                device_id_type=MESH,
            ).wait_recv()
            beside(d, k, False).start()

        each(half, relay)
    for d in range(1, n_dp):
        each(half, lambda k: beside(d, k, True).wait_recv())
    for p in range(n_dp):
        turned[:, p * count : (p + 1) * count] = merge_rows(feats[p], count).T
    each(every - 1, lambda k: shared(k + 1).wait_recv())
    total_grad = jnp.dot(
        turned[...], merge_rows(grads[...], every * bins), preferred_element_type=F32
    ).astype(BF16)
    channels = grow_ref.shape[1]
    grow_ref[...] = total_grad[:, 0:channels]
    gcol_ref[...] = total_grad[:, channels : 2 * channels]

    own.drain()
    for d in range(1, n_dp):
        each(half, lambda k: across(d, k).wait_send())
        each(half, lambda k: beside(d, k, False).wait_send())
    each(n_seq - 1, lambda k: scatter(k + 1).wait_send())
    each(every - 1, lambda k: share(k + 1).wait_send())


def on_device(
    n_dp,
    n_seq,
    tokens,
    query_weight,
    key_weight,
    value_weight,
    output_weight,
    row_weight,
    col_weight,
    pair_cotangent,
):
    rows, width = tokens.shape[1:]
    head = key_weight.shape[1]
    heads_wide = query_weight.shape[1]
    bins, count, channels = pair_cotangent.shape[1:]
    shard = key_weight.shape[0]
    vmem = pl.BlockSpec(memory_space=pltpu.VMEM)
    dma = pltpu.SemaphoreType.DMA
    both = lax.all_gather(
        jnp.concatenate([query_weight, output_weight], axis=1), "seq", axis=0, tiled=True
    )
    moves = copies_of(n_seq)
    normed, kv = pl.pallas_call(
        functools.partial(kv_kernel, n_dp, n_seq),
        out_shape=(
            jax.ShapeDtypeStruct((rows, width), BF16),
            jax.ShapeDtypeStruct((n_seq, rows, 2 * head), BF16),
        ),
        in_specs=[vmem] * 3,
        out_specs=(vmem, vmem),
        scratch_shapes=[
            pltpu.VMEM((n_seq, shard, 2 * head), BF16),
            dma((moves,)),
            dma((n_seq,)),
            dma((moves,)),
            dma((n_seq,)),
        ],
        cost_estimate=pl.CostEstimate(
            flops=4 * rows * width * head, bytes_accessed=64 * 2**20, transcendentals=rows
        ),
        compiler_params=pltpu.CompilerParams(
            collective_id=0, has_side_effects=True, vmem_limit_bytes=24 * 2**20
        ),
    )(tokens[0], key_weight, value_weight)
    every = n_dp * n_seq
    pair, grow, gcol = pl.pallas_call(
        functools.partial(main_kernel, n_dp, n_seq),
        out_shape=(
            jax.ShapeDtypeStruct((bins, count, channels), BF16),
            jax.ShapeDtypeStruct((width, channels), BF16),
            jax.ShapeDtypeStruct((width, channels), BF16),
        ),
        in_specs=[vmem, vmem, pl.BlockSpec(memory_space=pl.ANY), vmem, vmem, vmem],
        out_specs=(vmem, vmem, vmem),
        scratch_shapes=[
            pltpu.VMEM((width, heads_wide), BF16),
            pltpu.VMEM((width, heads_wide), BF16),
            pltpu.VMEM((rows, heads_wide), BF16),
            pltpu.VMEM((n_dp, n_seq, bins, width), BF16),
            pltpu.VMEM((n_seq, bins, channels), F32),
            pltpu.VMEM((n_seq, bins, channels), F32),
            pltpu.VMEM((every, bins, 2 * channels), BF16),
            pltpu.VMEM((width, n_dp * count), BF16),
            dma((2,)),
            dma((moves,)),
            dma((n_seq,)),
            dma((n_dp, n_seq // 2)),
            dma((n_dp, n_seq)),
            dma((n_dp, n_seq // 2)),
            dma((n_seq,)),
            dma((n_seq,)),
            dma((every,)),
            dma((every,)),
        ],
        compiler_params=pltpu.CompilerParams(
            collective_id=1, has_side_effects=True, vmem_limit_bytes=60 * 2**20
        ),
    )(normed, kv, both, row_weight, col_weight, pair_cotangent[0])
    return (pair[None], grow, gcol)


def solution(mesh):
    placed = (
        P("dp", "seq", None),
        P("seq", None),
        P("seq", None),
        P("seq", None),
        P("seq", None),
        P(),
        P(),
        P("dp", "seq", None, None),
    )
    return jax.shard_map(
        functools.partial(on_device, mesh.shape["dp"], mesh.shape["seq"]),
        mesh=mesh,
        in_specs=placed,
        out_specs=(P("dp", "seq", None, None), P(), P()),
        check_vma=False,
    )
```

```python
import functools
import math

import jax
import jax.numpy as jnp
from jax import lax
from jax.experimental import pallas as pl
from jax.experimental.pallas import tpu as pltpu
from jax.sharding import PartitionSpec as P

POOL = 16
LINE = 4
ORDER = (1, LINE - 1, *range(2, LINE - 1))
F32 = jnp.float32
BF16 = jnp.bfloat16
MESH = pl.DeviceIdType.MESH
LAST = (((1,), (1,)), ((), ()))


def merge_rows(block, rows):
    if block.shape[1] % 16 == 0:
        return block.reshape(rows, block.shape[2])
    return block.astype(F32).reshape(rows, block.shape[2]).astype(block.dtype)


class Where:
    def __init__(self, n_dp, n_seq):
        self.n_dp, self.n_seq = n_dp, n_seq
        self.mid = n_seq // (LINE * 2)
        self.dp, self.me = lax.axis_index("dp"), lax.axis_index("seq")
        self.core = self.me % 2
        self.y = (self.me // 2) % self.mid
        self.z = self.me // (2 * self.mid)

    def at(self, dz, dy, flip):
        z = (self.z + dz) % LINE
        y = (self.y + dy) % self.mid
        core = 1 - self.core if flip else self.core
        return (z * self.mid + y) * 2 + core


class Gather:
    def __init__(self, where, slot, send_sem, recv_sem):
        self.w, self.slot = where, slot
        self.send_sem, self.recv_sem = send_sem, recv_sem
        self.sent = []

    def push(self, block, peer):
        ref = self.slot(block)
        copy = pltpu.make_async_remote_copy(
            src_ref=ref,
            dst_ref=ref,
            send_sem=self.send_sem.at[len(self.sent)],
            recv_sem=self.recv_sem.at[block],
            device_id=(self.w.dp, peer),
            device_id_type=MESH,
        )
        copy.start()
        self.sent.append(copy)

    def arrived(self, block):
        ref = self.slot(block)
        pltpu.make_async_remote_copy(
            src_ref=ref,
            dst_ref=ref,
            send_sem=self.send_sem.at[0],
            recv_sem=self.recv_sem.at[block],
            device_id=(self.w.dp, self.w.me),
            device_id_type=MESH,
        ).wait_recv()

    def hold(self, block):
        pass

    def start(self):
        w = self.w
        for dz in ORDER:
            self.push(w.me, w.at(dz, 0, False))
        self.spread(0)

    def spread(self, dz):
        w = self.w
        block = w.at(dz, 0, False)
        for dy in range(1, w.mid):
            self.push(block, w.at(0, dy, False))
        if dz:
            self.hold(block)
        self.push(block, w.at(0, 0, True))

    def pass_line(self):
        for dz in ORDER:
            self.arrived(self.w.at(dz, 0, False))
            self.spread(dz)

    def pass_mid(self):
        w = self.w
        for dz in (0, *ORDER):
            for dy in range(1, w.mid):
                block = w.at(dz, dy, False)
                self.arrived(block)
                self.hold(block)
                self.push(block, w.at(0, 0, True))

    def pass_on(self):
        self.pass_line()
        self.pass_mid()

    def complete(self):
        w = self.w
        for dz in (0, *ORDER):
            for dy in range(w.mid):
                self.arrived(w.at(dz, dy, True))

    def drain(self):
        for copy in self.sent:
            copy.wait_send()


class Shared(Gather):
    def __init__(self, where, buf, sems):
        odd = where.dp % 2
        super().__init__(where, lambda s: buf.at[s, pl.ds(odd, 2)], sems[0], sems[1])
        self.buf, self.odd = buf, odd
        self.x_send, self.x_recv, self.s_send = sems[2:]
        self.crossed = []
        self.beside = []

    def third(self, block, piece):
        return self.buf.at[block, piece]

    def trade(self, block, piece, send_sem, dp, peer):
        ref = self.third(block, piece)
        return pltpu.make_async_remote_copy(
            src_ref=ref,
            dst_ref=ref,
            send_sem=send_sem,
            recv_sem=self.x_recv.at[block],
            device_id=(dp, peer),
            device_id_type=MESH,
        )

    def hold(self, block):
        w = self.w
        copy = self.trade(
            block, 2 * self.odd, self.x_send.at[len(self.crossed)], w.dp + 1 - 2 * self.odd, w.me
        )
        copy.start()
        self.crossed.append(copy)

    def pass_across(self):
        w = self.w
        for dy in range(w.mid):
            for dz in (0, *ORDER):
                block = w.at(dz, dy, False)
                send = self.s_send.at[len(self.beside)]
                copy = self.trade(block, 2 - 2 * self.odd, send, w.dp, w.at(0, 0, True))
                if dz or dy:
                    copy.wait_recv()
                copy.start()
                self.beside.append(copy)

    def complete(self):
        super().complete()
        w = self.w
        for dz in (0, *ORDER):
            for dy in range(w.mid):
                block = w.at(dz, dy, True)
                self.trade(
                    block, 2 - 2 * self.odd, self.s_send.at[0], w.dp, w.at(0, 0, True)
                ).wait_recv()

    def drain(self):
        for copy in self.sent + self.crossed + self.beside:
            copy.wait_send()


def copies_of(n_seq):
    mid = n_seq // (LINE * 2)
    return (LINE - 1) + LINE * (mid - 1) + LINE * mid


def shared_sems(n_seq):
    dma = pltpu.SemaphoreType.DMA
    half = n_seq // 2
    return [dma((copies_of(n_seq),)), dma((n_seq,)), dma((half,)), dma((n_seq,)), dma((half,))]


def main_kernel(
    n_dp,
    n_seq,
    tok_hbm,
    wq_hbm,
    wk_hbm,
    wv_hbm,
    wo_hbm,
    roww_hbm,
    colw_hbm,
    cot_hbm,
    rowp_ref,
    colp_ref,
    turned,
    grads,
    tok_ref,
    roww_ref,
    colw_ref,
    cot_ref,
    wkv_buf,
    wq_buf,
    wo_buf,
    kv_ref,
    att,
    feats,
    terms,
    parts,
    load_sem,
    k_send,
    k_recv,
    f_send,
    f_recv,
    x_send,
    x_recv,
    s_send,
    r_send,
    r_recv,
    g_send,
    g_recv,
    *weight_sems,
):
    w = Where(n_dp, n_seq)
    dp, me = w.dp, w.me
    every = n_dp * n_seq
    flat = dp * n_seq + me
    half = n_seq // 2
    head = wk_hbm.shape[2]
    heads_wide = wq_buf.shape[3]
    rows, width = tok_ref.shape

    sources = (
        (wk_hbm, wkv_buf.at[me, :, :, pl.ds(0, head)]),
        (wv_hbm, wkv_buf.at[me, :, :, pl.ds(head, head)]),
        (wq_hbm, wq_buf.at[me]),
        (tok_hbm, tok_ref),
        (wo_hbm, wo_buf.at[me]),
        (roww_hbm, roww_ref),
        (colw_hbm, colw_ref),
        (cot_hbm, cot_ref),
    )
    loads = [
        pltpu.make_async_copy(src, dst, load_sem.at[i]) for i, (src, dst) in enumerate(sources)
    ]
    for load in loads:
        load.start()

    barrier = pltpu.get_barrier_semaphore()

    def greet(t, unused):
        peer = (flat + t) % every
        pl.semaphore_signal(
            barrier, inc=1, device_id=(peer // n_seq, peer % n_seq), device_id_type=MESH
        )
        return unused

    lax.fori_loop(1, every, greet, 0)
    loads[0].wait()
    loads[1].wait()
    loads[2].wait()
    pl.semaphore_wait(barrier, every - 1)
    wkv = Shared(w, wkv_buf, weight_sems[0:5])
    wq = Shared(w, wq_buf, weight_sems[5:10])
    wo = Shared(w, wo_buf, weight_sems[10:15])
    wkv.start()
    wq.start()
    loads[3].wait()
    tok = tok_ref[...].astype(F32)
    normed = (tok * lax.rsqrt(jnp.mean(tok * tok, axis=1, keepdims=True) + 1e-06)).astype(BF16)
    wkv.pass_line()
    wkv.pass_mid()
    wkv.pass_across()
    wkv.complete()

    def whole(buf):
        return merge_rows(buf[...].reshape(n_seq * 3, buf.shape[2], buf.shape[3]), width)

    kv_ref[me] = jnp.dot(normed, whole(wkv_buf), preferred_element_type=F32).astype(BF16)
    blocks = Gather(w, lambda s: kv_ref.at[s], k_send, k_recv)
    blocks.start()
    wq.pass_line()
    blocks.pass_line()
    wq.pass_mid()
    blocks.pass_mid()
    wq.pass_across()
    wq.complete()
    loads[4].wait()
    wo.start()
    queries = jnp.dot(normed, whole(wq_buf), preferred_element_type=F32).astype(BF16)
    blocks.complete()
    relays = [wo.pass_line, wo.pass_mid, wo.pass_across]
    length = n_seq * rows
    keys = kv_ref[:, :, 0:head].reshape(length, head)
    values = kv_ref[:, :, head : 2 * head].reshape(length, head)
    factor = math.log2(math.e) / math.sqrt(head)
    for h in range(0, heads_wide // head, 2):
        both = jnp.concatenate(
            [queries[:, h * head : (h + 1) * head], queries[:, (h + 1) * head : (h + 2) * head]],
            axis=0,
        )
        scores = lax.dot_general(both, keys, LAST, preferred_element_type=F32)
        top = jnp.max(scores, axis=1, keepdims=True)
        weights = jnp.exp2((scores - top) * factor)
        total = jnp.sum(weights, axis=1, keepdims=True)
        out = jnp.dot(weights.astype(BF16), values, preferred_element_type=F32) / total
        out = out.astype(BF16)
        att[:, h * head : (h + 1) * head] = out[0:rows]
        att[:, (h + 1) * head : (h + 2) * head] = out[rows : 2 * rows]
        if relays:
            relays.pop(0)()
    for relay in relays:
        relay()
    wo.complete()
    update = lax.dot_general(att[...], whole(wo_buf), LAST, preferred_element_type=F32)
    bins = rows // POOL
    pooled = jnp.mean(update.reshape(bins, POOL, width), axis=1)
    scale = lax.rsqrt(jnp.mean(pooled * pooled, axis=1, keepdims=True) + 1e-06)
    feat = (pooled * scale).astype(BF16)
    feats[dp, me] = feat
    for load in loads[5:]:
        load.wait()

    own = Gather(w, lambda s: feats.at[dp, s], f_send, f_recv)
    own.start()
    row_proj = jnp.dot(feat, roww_ref[...], preferred_element_type=F32).astype(BF16)
    own.pass_on()

    def across(d, k):
        slot = 2 * k + w.core
        ref = feats.at[dp, slot]
        return pltpu.make_async_remote_copy(
            src_ref=ref,
            dst_ref=ref,
            send_sem=x_send.at[d, k],
            recv_sem=x_recv.at[dp, slot],
            device_id=((dp + d) % n_dp, me),
            device_id_type=MESH,
        )

    def beside(d, k, flip):
        slot = 2 * k + (1 - w.core if flip else w.core)
        other = (dp + d) % n_dp
        ref = feats.at[other, slot]
        return pltpu.make_async_remote_copy(
            src_ref=ref,
            dst_ref=ref,
            send_sem=s_send.at[d, k],
            recv_sem=x_recv.at[other, slot],
            device_id=(dp, w.at(0, 0, True)),
            device_id_type=MESH,
        )

    def each(count, act):
        def step(k, unused):
            act(k)
            return unused

        lax.fori_loop(0, count, step, 0)

    for d in range(1, n_dp):
        each(half, lambda k: across(d, k).start())
    own.complete()

    count = n_seq * bins
    mine = merge_rows(feats[dp], count)
    col_proj = jnp.dot(mine, colw_ref[...], preferred_element_type=F32).astype(BF16)
    row_wide = row_proj.astype(F32)
    col_wide = col_proj.astype(F32)
    sums = jnp.zeros(col_wide.shape, F32)
    for i in range(bins):
        sums = sums + cot_ref[i].astype(F32) * row_wide[i : i + 1, :]
    terms[...] = sums.reshape(terms.shape)

    def scatter(t):
        peer = (me + t) % n_seq
        return pltpu.make_async_remote_copy(
            src_ref=terms.at[peer],
            dst_ref=parts.at[me],
            send_sem=r_send.at[t],
            recv_sem=r_recv.at[me],
            device_id=(dp, peer),
            device_id_type=MESH,
        )

    def scattered(t):
        peer = (me + t) % n_seq
        return pltpu.make_async_remote_copy(
            src_ref=terms.at[me],
            dst_ref=parts.at[peer],
            send_sem=r_send.at[t],
            recv_sem=r_recv.at[peer],
            device_id=(dp, peer),
            device_id_type=MESH,
        )

    each(n_seq - 1, lambda k: scatter(k + 1).start())
    parts[me] = terms[me]
    rowp_ref[...] = row_wide
    colp_ref[...] = col_wide
    row_list = []
    for i in range(bins):
        row_list.append(jnp.sum(cot_ref[i].astype(F32) * col_wide, axis=0, keepdims=True))
    row_grad = jnp.concatenate(row_list, axis=0)
    each(n_seq - 1, lambda k: scattered(k + 1).wait_recv())
    col_grad = jnp.sum(parts[...], axis=0)
    grads[flat] = jnp.concatenate([row_grad, col_grad], axis=1).astype(BF16)

    def share(t):
        peer = (flat + t) % every
        return pltpu.make_async_remote_copy(
            src_ref=grads.at[flat],
            dst_ref=grads.at[flat],
            send_sem=g_send.at[t],
            recv_sem=g_recv.at[flat],
            device_id=(peer // n_seq, peer % n_seq),
            device_id_type=MESH,
        )

    def shared(t):
        peer = (flat + t) % every
        return pltpu.make_async_remote_copy(
            src_ref=grads.at[peer],
            dst_ref=grads.at[peer],
            send_sem=g_send.at[t],
            recv_sem=g_recv.at[peer],
            device_id=(dp, me),
            device_id_type=MESH,
        )

    each(every - 1, lambda k: share(k + 1).start())

    for d in range(1, n_dp):

        def relay(k):
            slot = 2 * k + w.core
            other = (dp + d) % n_dp
            ref = feats.at[other, slot]
            pltpu.make_async_remote_copy(
                src_ref=ref,
                dst_ref=ref,
                send_sem=s_send.at[d, k],
                recv_sem=x_recv.at[other, slot],
                device_id=(dp, me),
                device_id_type=MESH,
            ).wait_recv()
            beside(d, k, False).start()

        each(half, relay)
    for d in range(1, n_dp):
        each(half, lambda k: beside(d, k, True).wait_recv())
    for p in range(n_dp):
        turned[:, p * count : (p + 1) * count] = merge_rows(feats[p], count).T
    each(every - 1, lambda k: shared(k + 1).wait_recv())

    for weights in (wkv, wq, wo):
        weights.drain()
    blocks.drain()
    own.drain()
    for d in range(1, n_dp):
        each(half, lambda k: across(d, k).wait_send())
        each(half, lambda k: beside(d, k, False).wait_send())
    each(n_seq - 1, lambda k: scatter(k + 1).wait_send())
    each(every - 1, lambda k: share(k + 1).wait_send())


def tail_kernel(rowp_ref, colp_ref, turned, grads, pair_ref, grow_ref, gcol_ref):
    for i in range(rowp_ref.shape[0]):
        pair_ref[i] = (rowp_ref[i : i + 1, :] * colp_ref[...]).astype(BF16)
    total = jnp.dot(
        turned[...], merge_rows(grads[...], turned.shape[1]), preferred_element_type=F32
    ).astype(BF16)
    channels = grow_ref.shape[1]
    grow_ref[...] = total[:, 0:channels]
    gcol_ref[...] = total[:, channels : 2 * channels]


def on_device(
    n_dp,
    n_seq,
    tokens,
    query_weight,
    key_weight,
    value_weight,
    output_weight,
    row_weight,
    col_weight,
    pair_cotangent,
):
    rows, width = tokens.shape[1:]
    head = key_weight.shape[1]
    heads_wide = query_weight.shape[1]
    bins, count, channels = pair_cotangent.shape[1:]
    third = key_weight.shape[0] // 3
    vmem = pl.BlockSpec(memory_space=pltpu.VMEM)
    hbm = pl.BlockSpec(memory_space=pltpu.HBM)
    dma = pltpu.SemaphoreType.DMA
    moves = copies_of(n_seq)
    every = n_dp * n_seq
    grant = (30 if every <= 32 else 60) * 2**20
    kept = pl.pallas_call(
        functools.partial(main_kernel, n_dp, n_seq),
        out_shape=(
            jax.ShapeDtypeStruct((bins, channels), F32),
            jax.ShapeDtypeStruct((count, channels), F32),
            jax.ShapeDtypeStruct((width, n_dp * count), BF16),
            jax.ShapeDtypeStruct((every, bins, 2 * channels), BF16),
        ),
        in_specs=[hbm] * 8,
        out_specs=(vmem,) * 4,
        scratch_shapes=[
            pltpu.VMEM((rows, width), BF16),
            pltpu.VMEM((width, channels), BF16),
            pltpu.VMEM((width, channels), BF16),
            pltpu.VMEM((bins, count, channels), BF16),
            pltpu.VMEM((n_seq, 3, third, 2 * head), BF16),
            pltpu.VMEM((n_seq, 3, third, heads_wide), BF16),
            pltpu.VMEM((n_seq, 3, third, heads_wide), BF16),
            pltpu.VMEM((n_seq, rows, 2 * head), BF16),
            pltpu.VMEM((rows, heads_wide), BF16),
            pltpu.VMEM((n_dp, n_seq, bins, width), BF16),
            pltpu.VMEM((n_seq, bins, channels), F32),
            pltpu.VMEM((n_seq, bins, channels), F32),
            dma((8,)),
            dma((moves,)),
            dma((n_seq,)),
            dma((moves,)),
            dma((n_seq,)),
            dma((n_dp, n_seq // 2)),
            dma((n_dp, n_seq)),
            dma((n_dp, n_seq // 2)),
            dma((n_seq,)),
            dma((n_seq,)),
            dma((every,)),
            dma((every,)),
            *shared_sems(n_seq),
            *shared_sems(n_seq),
            *shared_sems(n_seq),
        ],
        compiler_params=pltpu.CompilerParams(
            collective_id=0, has_side_effects=True, vmem_limit_bytes=grant
        ),
    )(
        tokens[0],
        query_weight.reshape(3, third, heads_wide),
        key_weight.reshape(3, third, head),
        value_weight.reshape(3, third, head),
        output_weight.reshape(3, third, heads_wide),
        row_weight,
        col_weight,
        pair_cotangent[0],
    )
    pair, grow, gcol = pl.pallas_call(
        tail_kernel,
        out_shape=(
            jax.ShapeDtypeStruct((bins, count, channels), BF16),
            jax.ShapeDtypeStruct((width, channels), BF16),
            jax.ShapeDtypeStruct((width, channels), BF16),
        ),
        in_specs=[vmem] * 4,
        out_specs=(vmem,) * 3,
        compiler_params=pltpu.CompilerParams(vmem_limit_bytes=grant),
    )(*kept)
    return (pair[None], grow, gcol)


def solution(mesh):
    placed = (
        P("dp", "seq", None),
        P("seq", None),
        P("seq", None),
        P("seq", None),
        P("seq", None),
        P(),
        P(),
        P("dp", "seq", None, None),
    )
    return jax.shard_map(
        functools.partial(on_device, mesh.shape["dp"], mesh.shape["seq"]),
        mesh=mesh,
        in_specs=placed,
        out_specs=(P("dp", "seq", None, None), P(), P()),
        check_vma=False,
    )
```

```python
import functools
import math

import jax
import jax.numpy as jnp
from jax import lax
from jax.experimental import pallas as pl
from jax.experimental.pallas import tpu as pltpu
from jax.sharding import PartitionSpec as P

POOL = 16
LINE = 4
ORDER = (1, LINE - 1, *range(2, LINE - 1))
F32 = jnp.float32
BF16 = jnp.bfloat16
MESH = pl.DeviceIdType.MESH
LAST = (((1,), (1,)), ((), ()))


def merge_rows(block, rows):
    if block.shape[1] % 16 == 0:
        return block.reshape(rows, block.shape[2])
    return block.astype(F32).reshape(rows, block.shape[2]).astype(block.dtype)


class Where:
    def __init__(self, n_dp, n_seq):
        self.n_dp, self.n_seq = n_dp, n_seq
        self.mid = n_seq // (LINE * 2)
        self.dp, self.me = lax.axis_index("dp"), lax.axis_index("seq")
        self.core = self.me % 2
        self.y = (self.me // 2) % self.mid
        self.z = self.me // (2 * self.mid)

    def at(self, dz, dy, flip):
        z = (self.z + dz) % LINE
        y = (self.y + dy) % self.mid
        core = 1 - self.core if flip else self.core
        return (z * self.mid + y) * 2 + core


class Gather:
    def __init__(self, where, slot, send_sem, recv_sem):
        self.w, self.slot = where, slot
        self.send_sem, self.recv_sem = send_sem, recv_sem
        self.sent = []

    def push(self, block, peer):
        ref = self.slot(block)
        copy = pltpu.make_async_remote_copy(
            src_ref=ref,
            dst_ref=ref,
            send_sem=self.send_sem.at[len(self.sent)],
            recv_sem=self.recv_sem.at[block],
            device_id=(self.w.dp, peer),
            device_id_type=MESH,
        )
        copy.start()
        self.sent.append(copy)

    def arrived(self, block):
        ref = self.slot(block)
        pltpu.make_async_remote_copy(
            src_ref=ref,
            dst_ref=ref,
            send_sem=self.send_sem.at[0],
            recv_sem=self.recv_sem.at[block],
            device_id=(self.w.dp, self.w.me),
            device_id_type=MESH,
        ).wait_recv()

    def hold(self, block):
        pass

    def start(self):
        w = self.w
        for dz in ORDER:
            self.push(w.me, w.at(dz, 0, False))
        self.spread(0)

    def spread(self, dz):
        w = self.w
        block = w.at(dz, 0, False)
        for dy in range(1, w.mid):
            self.push(block, w.at(0, dy, False))
        if dz:
            self.hold(block)
        self.push(block, w.at(0, 0, True))

    def pass_line(self):
        for dz in ORDER:
            self.arrived(self.w.at(dz, 0, False))
            self.spread(dz)

    def pass_mid(self):
        w = self.w
        for dz in (0, *ORDER):
            for dy in range(1, w.mid):
                block = w.at(dz, dy, False)
                self.arrived(block)
                self.hold(block)
                self.push(block, w.at(0, 0, True))

    def pass_on(self):
        self.pass_line()
        self.pass_mid()

    def complete(self):
        w = self.w
        for dz in (0, *ORDER):
            for dy in range(w.mid):
                self.arrived(w.at(dz, dy, True))

    def drain(self):
        for copy in self.sent:
            copy.wait_send()


class Shared(Gather):
    def __init__(self, where, buf, sems):
        odd = where.dp % 2
        super().__init__(where, lambda s: buf.at[s, pl.ds(odd, 2)], sems[0], sems[1])
        self.buf, self.odd = buf, odd
        self.x_send, self.x_recv, self.s_send = sems[2:]
        self.crossed = []
        self.beside = []

    def third(self, block, piece):
        return self.buf.at[block, piece]

    def trade(self, block, piece, send_sem, dp, peer):
        ref = self.third(block, piece)
        return pltpu.make_async_remote_copy(
            src_ref=ref,
            dst_ref=ref,
            send_sem=send_sem,
            recv_sem=self.x_recv.at[block],
            device_id=(dp, peer),
            device_id_type=MESH,
        )

    def hold(self, block):
        w = self.w
        copy = self.trade(
            block, 2 * self.odd, self.x_send.at[len(self.crossed)], w.dp + 1 - 2 * self.odd, w.me
        )
        copy.start()
        self.crossed.append(copy)

    def pass_across(self):
        w = self.w
        for dy in range(w.mid):
            for dz in (0, *ORDER):
                block = w.at(dz, dy, False)
                send = self.s_send.at[len(self.beside)]
                copy = self.trade(block, 2 - 2 * self.odd, send, w.dp, w.at(0, 0, True))
                if dz or dy:
                    copy.wait_recv()
                copy.start()
                self.beside.append(copy)

    def complete(self):
        super().complete()
        w = self.w
        for dz in (0, *ORDER):
            for dy in range(w.mid):
                block = w.at(dz, dy, True)
                self.trade(
                    block, 2 - 2 * self.odd, self.s_send.at[0], w.dp, w.at(0, 0, True)
                ).wait_recv()

    def drain(self):
        for copy in self.sent + self.crossed + self.beside:
            copy.wait_send()


def copies_of(n_seq):
    mid = n_seq // (LINE * 2)
    return (LINE - 1) + LINE * (mid - 1) + LINE * mid


def shared_sems(n_seq):
    dma = pltpu.SemaphoreType.DMA
    half = n_seq // 2
    return [dma((copies_of(n_seq),)), dma((n_seq,)), dma((half,)), dma((n_seq,)), dma((half,))]


def main_kernel(
    n_dp,
    n_seq,
    tok_hbm,
    wq_hbm,
    wk_hbm,
    wv_hbm,
    wo_hbm,
    roww_hbm,
    colw_hbm,
    cot_hbm,
    rowp_out,
    colp_out,
    turned_out,
    grads_out,
    rowp_ref,
    colp_ref,
    turned,
    grads,
    tok_ref,
    roww_ref,
    colw_ref,
    cot_ref,
    wkv_buf,
    wq_buf,
    wo_ref,
    kv_ref,
    att,
    binned,
    pooled_ref,
    terms,
    parts,
    load_sem,
    save_sem,
    k_send,
    k_recv,
    b_send,
    b_recv,
    f_send,
    f_recv,
    x_send,
    x_recv,
    s_send,
    r_send,
    r_recv,
    g_send,
    g_recv,
    *weight_sems,
):
    w = Where(n_dp, n_seq)
    dp, me = w.dp, w.me
    every = n_dp * n_seq
    flat = dp * n_seq + me
    head = wk_hbm.shape[2]
    heads_wide = wq_buf.shape[3]
    rows, width = tok_ref.shape

    sources = (
        (wk_hbm, wkv_buf.at[me, :, :, pl.ds(0, head)]),
        (wv_hbm, wkv_buf.at[me, :, :, pl.ds(head, head)]),
        (wq_hbm, wq_buf.at[me]),
        (tok_hbm, tok_ref),
        (wo_hbm, wo_ref),
        (roww_hbm, roww_ref),
        (colw_hbm, colw_ref),
        (cot_hbm, cot_ref),
    )
    loads = [
        pltpu.make_async_copy(src, dst, load_sem.at[i]) for i, (src, dst) in enumerate(sources)
    ]
    for load in loads:
        load.start()

    barrier = pltpu.get_barrier_semaphore()

    def greet(t, unused):
        peer = (flat + t) % every
        pl.semaphore_signal(
            barrier, inc=1, device_id=(peer // n_seq, peer % n_seq), device_id_type=MESH
        )
        return unused

    lax.fori_loop(1, every, greet, 0)
    loads[0].wait()
    loads[1].wait()
    loads[2].wait()
    pl.semaphore_wait(barrier, every - 1)
    wkv = Shared(w, wkv_buf, weight_sems[0:5])
    wq = Shared(w, wq_buf, weight_sems[5:10])
    wkv.start()
    wq.start()
    loads[3].wait()
    tok = tok_ref[...].astype(F32)
    normed = (tok * lax.rsqrt(jnp.mean(tok * tok, axis=1, keepdims=True) + 1e-06)).astype(BF16)
    wkv.pass_line()
    wkv.pass_mid()
    wkv.pass_across()
    wkv.complete()

    def whole(buf):
        return merge_rows(buf[...].reshape(n_seq * 3, buf.shape[2], buf.shape[3]), width)

    kv_ref[me] = jnp.dot(normed, whole(wkv_buf), preferred_element_type=F32).astype(BF16)
    blocks = Gather(w, lambda s: kv_ref.at[s], k_send, k_recv)
    blocks.start()
    wq.pass_line()
    blocks.pass_line()
    wq.pass_mid()
    blocks.pass_mid()
    wq.pass_across()
    wq.complete()
    queries = jnp.dot(normed, whole(wq_buf), preferred_element_type=F32).astype(BF16)
    blocks.complete()
    length = n_seq * rows
    keys = kv_ref[:, :, 0:head].reshape(length, head)
    values = kv_ref[:, :, head : 2 * head].reshape(length, head)
    factor = math.log2(math.e) / math.sqrt(head)
    for h in range(0, heads_wide // head, 2):
        both = jnp.concatenate(
            [queries[:, h * head : (h + 1) * head], queries[:, (h + 1) * head : (h + 2) * head]],
            axis=0,
        )
        scores = lax.dot_general(both, keys, LAST, preferred_element_type=F32)
        top = jnp.max(scores, axis=1, keepdims=True)
        weights = jnp.exp2((scores - top) * factor)
        total = jnp.sum(weights, axis=1, keepdims=True)
        out = jnp.dot(weights.astype(BF16), values, preferred_element_type=F32) / total
        out = out.astype(BF16)
        att[:, h * head : (h + 1) * head] = out[0:rows]
        att[:, (h + 1) * head : (h + 2) * head] = out[rows : 2 * rows]
    bins = rows // POOL
    count = n_seq * bins
    binned[me] = jnp.sum(att[...].astype(F32).reshape(bins, POOL, heads_wide), axis=1)
    for load in loads[4:]:
        load.wait()
    attended = Gather(w, lambda s: binned.at[s], b_send, b_recv)
    attended.start()
    attended.pass_on()
    attended.complete()
    summed = binned[...].reshape(count, heads_wide)
    high = summed.astype(BF16)
    low = (summed - high.astype(F32)).astype(BF16)
    update = lax.dot_general(wo_ref[...], high, LAST, preferred_element_type=F32)
    update = update + lax.dot_general(wo_ref[...], low, LAST, preferred_element_type=F32)
    pooled_ref[me] = update * (1.0 / POOL)
    own = Gather(w, lambda s: pooled_ref.at[s], f_send, f_recv)
    own.start()
    own.pass_on()
    own.complete()
    pooled = pooled_ref[...].reshape(width, count)
    scale = lax.rsqrt(jnp.mean(pooled * pooled, axis=0, keepdims=True) + 1e-06)
    feat = (pooled * scale).astype(BF16)
    turned[dp] = feat
    share_rows = width // 2

    def piece(p, core):
        return turned.at[p, pl.ds(pl.multiple_of(core * share_rows, share_rows), share_rows)]

    def across(d):
        ref = piece(dp, w.core)
        return pltpu.make_async_remote_copy(
            src_ref=ref,
            dst_ref=ref,
            send_sem=x_send.at[d],
            recv_sem=x_recv.at[dp, w.core],
            device_id=((dp + d) % n_dp, me),
            device_id_type=MESH,
        )

    def beside(d, core):
        other = (dp + d) % n_dp
        ref = piece(other, core)
        return pltpu.make_async_remote_copy(
            src_ref=ref,
            dst_ref=ref,
            send_sem=s_send.at[d],
            recv_sem=x_recv.at[other, core],
            device_id=(dp, w.at(0, 0, True)),
            device_id_type=MESH,
        )

    def each(total, act):
        def step(k, unused):
            act(k)
            return unused

        lax.fori_loop(0, total, step, 0)

    for d in range(1, n_dp):
        across(d).start()

    def save(src, dst, i):
        copy = pltpu.make_async_copy(src, dst, save_sem.at[i])
        copy.start()
        return copy

    saves = [save(turned.at[dp], turned_out.at[dp], 0)]
    feat_rows = feat.T
    row_all = jnp.dot(feat_rows, roww_ref[...], preferred_element_type=F32).astype(BF16)
    col_proj = jnp.dot(feat_rows, colw_ref[...], preferred_element_type=F32).astype(BF16)
    rowp_ref[...] = row_all.astype(F32).reshape(rowp_ref.shape)
    col_wide = col_proj.astype(F32)
    colp_ref[...] = col_wide
    saves.append(save(rowp_ref.at[me], rowp_out, 1))
    saves.append(save(colp_ref, colp_out, 2))
    row_wide = rowp_ref[me]
    sums = jnp.zeros(col_wide.shape, F32)
    for i in range(bins):
        sums = sums + cot_ref[i].astype(F32) * row_wide[i : i + 1, :]
    terms[...] = sums.reshape(terms.shape)

    def scatter(t):
        peer = (me + t) % n_seq
        return pltpu.make_async_remote_copy(
            src_ref=terms.at[peer],
            dst_ref=parts.at[me],
            send_sem=r_send.at[t],
            recv_sem=r_recv.at[me],
            device_id=(dp, peer),
            device_id_type=MESH,
        )

    def scattered(t):
        peer = (me + t) % n_seq
        return pltpu.make_async_remote_copy(
            src_ref=terms.at[me],
            dst_ref=parts.at[peer],
            send_sem=r_send.at[t],
            recv_sem=r_recv.at[peer],
            device_id=(dp, peer),
            device_id_type=MESH,
        )

    each(n_seq - 1, lambda k: scatter(k + 1).start())
    parts[me] = terms[me]
    row_list = []
    for i in range(bins):
        row_list.append(jnp.sum(cot_ref[i].astype(F32) * col_wide, axis=0, keepdims=True))
    row_grad = jnp.concatenate(row_list, axis=0)
    each(n_seq - 1, lambda k: scattered(k + 1).wait_recv())
    col_grad = jnp.sum(parts[...], axis=0)
    grads[flat] = jnp.concatenate([row_grad, col_grad], axis=1).astype(BF16)

    def share(t):
        peer = (flat + t) % every
        return pltpu.make_async_remote_copy(
            src_ref=grads.at[flat],
            dst_ref=grads.at[flat],
            send_sem=g_send.at[t],
            recv_sem=g_recv.at[flat],
            device_id=(peer // n_seq, peer % n_seq),
            device_id_type=MESH,
        )

    def shared(t):
        peer = (flat + t) % every
        return pltpu.make_async_remote_copy(
            src_ref=grads.at[peer],
            dst_ref=grads.at[peer],
            send_sem=g_send.at[t],
            recv_sem=g_recv.at[peer],
            device_id=(dp, me),
            device_id_type=MESH,
        )

    each(every - 1, lambda k: share(k + 1).start())

    for d in range(1, n_dp):
        beside(d, w.core).wait_recv()
        beside(d, w.core).start()
    for d in range(1, n_dp):
        beside(d, 1 - w.core).wait_recv()
        other = (dp + d) % n_dp
        saves.append(save(turned.at[other], turned_out.at[other], 3 + d))
    each(every - 1, lambda k: shared(k + 1).wait_recv())
    saves.append(save(grads, grads_out, 3))
    for weights in (wkv, wq, blocks, attended, own):
        weights.drain()
    for d in range(1, n_dp):
        across(d).wait_send()
        beside(d, w.core).wait_send()
    each(n_seq - 1, lambda k: scatter(k + 1).wait_send())
    each(every - 1, lambda k: share(k + 1).wait_send())
    for copy in saves:
        copy.wait()


def tail_kernel(rowp_ref, colp_ref, turned, grads, pair_ref, grow_ref, gcol_ref):
    for i in range(rowp_ref.shape[0]):
        pair_ref[i] = (rowp_ref[i : i + 1, :] * colp_ref[...]).astype(BF16)
    n_dp, width, count = turned.shape
    whole = merge_rows(grads[...], n_dp * count)
    total = jnp.zeros((width, whole.shape[1]), F32)
    for p in range(n_dp):
        part = whole[p * count : (p + 1) * count]
        total = total + jnp.dot(turned[p], part, preferred_element_type=F32)
    total = total.astype(BF16)
    channels = grow_ref.shape[1]
    grow_ref[...] = total[:, 0:channels]
    gcol_ref[...] = total[:, channels : 2 * channels]


def on_device(
    n_dp,
    n_seq,
    tokens,
    query_weight,
    key_weight,
    value_weight,
    output_weight,
    row_weight,
    col_weight,
    pair_cotangent,
):
    rows, width = tokens.shape[1:]
    head = key_weight.shape[1]
    heads_wide = query_weight.shape[1]
    bins, count, channels = pair_cotangent.shape[1:]
    third = key_weight.shape[0] // 3
    vmem = pl.BlockSpec(memory_space=pltpu.VMEM)
    hbm = pl.BlockSpec(memory_space=pltpu.HBM)
    dma = pltpu.SemaphoreType.DMA
    moves = copies_of(n_seq)
    every = n_dp * n_seq
    grant = 60 * 2**20
    kept = pl.pallas_call(
        functools.partial(main_kernel, n_dp, n_seq),
        out_shape=(
            jax.ShapeDtypeStruct((bins, channels), F32),
            jax.ShapeDtypeStruct((count, channels), F32),
            jax.ShapeDtypeStruct((n_dp, width, count), BF16),
            jax.ShapeDtypeStruct((every, bins, 2 * channels), BF16),
        ),
        in_specs=[hbm] * 8,
        out_specs=(hbm,) * 4,
        scratch_shapes=[
            pltpu.VMEM((n_seq, bins, channels), F32),
            pltpu.VMEM((count, channels), F32),
            pltpu.VMEM((n_dp, width, count), BF16),
            pltpu.VMEM((every, bins, 2 * channels), BF16),
            pltpu.VMEM((rows, width), BF16),
            pltpu.VMEM((width, channels), BF16),
            pltpu.VMEM((width, channels), BF16),
            pltpu.VMEM((bins, count, channels), BF16),
            pltpu.VMEM((n_seq, 3, third, 2 * head), BF16),
            pltpu.VMEM((n_seq, 3, third, heads_wide), BF16),
            pltpu.VMEM(output_weight.shape, BF16),
            pltpu.VMEM((n_seq, rows, 2 * head), BF16),
            pltpu.VMEM((rows, heads_wide), BF16),
            pltpu.VMEM((n_seq, bins, heads_wide), F32),
            pltpu.VMEM((n_seq, 3 * third, count), F32),
            pltpu.VMEM((n_seq, bins, channels), F32),
            pltpu.VMEM((n_seq, bins, channels), F32),
            dma((8,)),
            dma((3 + n_dp,)),
            *[dma((moves,)), dma((n_seq,))] * 3,
            dma((n_dp,)),
            dma((n_dp, 2)),
            dma((n_dp,)),
            dma((n_seq,)),
            dma((n_seq,)),
            dma((every,)),
            dma((every,)),
            *shared_sems(n_seq),
            *shared_sems(n_seq),
        ],
        compiler_params=pltpu.CompilerParams(
            collective_id=0, has_side_effects=True, vmem_limit_bytes=grant
        ),
    )(
        tokens[0],
        query_weight.reshape(3, third, heads_wide),
        key_weight.reshape(3, third, head),
        value_weight.reshape(3, third, head),
        output_weight,
        row_weight,
        col_weight,
        pair_cotangent[0],
    )
    pair, grow, gcol = pl.pallas_call(
        tail_kernel,
        out_shape=(
            jax.ShapeDtypeStruct((bins, count, channels), BF16),
            jax.ShapeDtypeStruct((width, channels), BF16),
            jax.ShapeDtypeStruct((width, channels), BF16),
        ),
        in_specs=[vmem] * 4,
        out_specs=(vmem,) * 3,
        compiler_params=pltpu.CompilerParams(vmem_limit_bytes=grant),
    )(*kept)
    return (pair[None], grow, gcol)


def solution(mesh):
    placed = (
        P("dp", "seq", None),
        P("seq", None),
        P("seq", None),
        P("seq", None),
        P("seq", None),
        P(),
        P(),
        P("dp", "seq", None, None),
    )
    return jax.shard_map(
        functools.partial(on_device, mesh.shape["dp"], mesh.shape["seq"]),
        mesh=mesh,
        in_specs=placed,
        out_specs=(P("dp", "seq", None, None), P(), P()),
        check_vma=False,
    )
```

```python
import functools
import math

import jax
import jax.numpy as jnp
from jax import lax
from jax.experimental import pallas as pl
from jax.experimental.pallas import tpu as pltpu
from jax.sharding import PartitionSpec as P

POOL = 16
LINE = 4
ORDER = (1, LINE - 1, *range(2, LINE - 1))
F32 = jnp.float32
BF16 = jnp.bfloat16
MESH = pl.DeviceIdType.MESH
LAST = (((1,), (1,)), ((), ()))


def merge_rows(block, rows):
    if block.shape[1] % 16 == 0:
        return block.reshape(rows, block.shape[2])
    return block.astype(F32).reshape(rows, block.shape[2]).astype(block.dtype)


class Where:
    def __init__(self, n_dp, n_seq):
        self.n_dp, self.n_seq = n_dp, n_seq
        self.mid = n_seq // (LINE * 2)
        self.dp, self.me = lax.axis_index("dp"), lax.axis_index("seq")
        self.core = self.me % 2
        self.y = (self.me // 2) % self.mid
        self.z = self.me // (2 * self.mid)

    def at(self, dz, dy, flip):
        z = (self.z + dz) % LINE
        y = (self.y + dy) % self.mid
        core = 1 - self.core if flip else self.core
        return (z * self.mid + y) * 2 + core


class Gather:
    def __init__(self, where, slot, send_sem, recv_sem):
        self.w, self.slot = where, slot
        self.send_sem, self.recv_sem = send_sem, recv_sem
        self.sent = []

    def push(self, block, peer):
        ref = self.slot(block)
        copy = pltpu.make_async_remote_copy(
            src_ref=ref,
            dst_ref=ref,
            send_sem=self.send_sem.at[len(self.sent)],
            recv_sem=self.recv_sem.at[block],
            device_id=(self.w.dp, peer),
            device_id_type=MESH,
        )
        copy.start()
        self.sent.append(copy)

    def arrived(self, block):
        ref = self.slot(block)
        pltpu.make_async_remote_copy(
            src_ref=ref,
            dst_ref=ref,
            send_sem=self.send_sem.at[0],
            recv_sem=self.recv_sem.at[block],
            device_id=(self.w.dp, self.w.me),
            device_id_type=MESH,
        ).wait_recv()

    def hold(self, block):
        pass

    def start(self):
        w = self.w
        for dz in ORDER:
            self.push(w.me, w.at(dz, 0, False))
        self.spread(0)

    def spread(self, dz):
        w = self.w
        block = w.at(dz, 0, False)
        for dy in range(1, w.mid):
            self.push(block, w.at(0, dy, False))
        if dz:
            self.hold(block)
        self.push(block, w.at(0, 0, True))

    def pass_line(self):
        for dz in ORDER:
            self.arrived(self.w.at(dz, 0, False))
            self.spread(dz)

    def pass_mid(self):
        w = self.w
        for dz in (0, *ORDER):
            for dy in range(1, w.mid):
                block = w.at(dz, dy, False)
                self.arrived(block)
                self.hold(block)
                self.push(block, w.at(0, 0, True))

    def pass_on(self):
        self.pass_line()
        self.pass_mid()

    def complete(self):
        w = self.w
        for dz in (0, *ORDER):
            for dy in range(w.mid):
                self.arrived(w.at(dz, dy, True))

    def drain(self):
        for copy in self.sent:
            copy.wait_send()


class Shared(Gather):
    def __init__(self, where, buf, sems):
        odd = where.dp % 2
        super().__init__(where, lambda s: buf.at[s, pl.ds(odd, 2)], sems[0], sems[1])
        self.buf, self.odd = buf, odd
        self.x_send, self.x_recv, self.s_send = sems[2:]
        self.crossed = []
        self.beside = []

    def third(self, block, piece):
        return self.buf.at[block, piece]

    def trade(self, block, piece, send_sem, dp, peer):
        ref = self.third(block, piece)
        return pltpu.make_async_remote_copy(
            src_ref=ref,
            dst_ref=ref,
            send_sem=send_sem,
            recv_sem=self.x_recv.at[block],
            device_id=(dp, peer),
            device_id_type=MESH,
        )

    def hold(self, block):
        w = self.w
        copy = self.trade(
            block, 2 * self.odd, self.x_send.at[len(self.crossed)], w.dp + 1 - 2 * self.odd, w.me
        )
        copy.start()
        self.crossed.append(copy)

    def pass_across(self):
        w = self.w
        for dy in range(w.mid):
            for dz in (0, *ORDER):
                block = w.at(dz, dy, False)
                send = self.s_send.at[len(self.beside)]
                copy = self.trade(block, 2 - 2 * self.odd, send, w.dp, w.at(0, 0, True))
                if dz or dy:
                    copy.wait_recv()
                copy.start()
                self.beside.append(copy)

    def complete(self):
        super().complete()
        w = self.w
        for dz in (0, *ORDER):
            for dy in range(w.mid):
                block = w.at(dz, dy, True)
                self.trade(
                    block, 2 - 2 * self.odd, self.s_send.at[0], w.dp, w.at(0, 0, True)
                ).wait_recv()

    def drain(self):
        for copy in self.sent + self.crossed + self.beside:
            copy.wait_send()


def copies_of(n_seq):
    mid = n_seq // (LINE * 2)
    return (LINE - 1) + LINE * (mid - 1) + LINE * mid


def shared_sems(n_seq):
    dma = pltpu.SemaphoreType.DMA
    half = n_seq // 2
    return [dma((copies_of(n_seq),)), dma((n_seq,)), dma((half,)), dma((n_seq,)), dma((half,))]


def main_kernel(
    n_dp,
    n_seq,
    tok_hbm,
    wq_hbm,
    wk_hbm,
    wv_hbm,
    wo_hbm,
    roww_hbm,
    colw_hbm,
    cot_hbm,
    rowp_out,
    colp_out,
    turned_out,
    grads_out,
    rowp_ref,
    colp_ref,
    turned,
    grads,
    tok_ref,
    roww_ref,
    colw_ref,
    cot_ref,
    wkv_buf,
    wq_buf,
    wo_ref,
    kv_ref,
    att,
    binned,
    pooled_ref,
    terms,
    parts,
    load_sem,
    save_sem,
    k_send,
    k_recv,
    b_send,
    b_recv,
    f_send,
    f_recv,
    x_send,
    x_recv,
    s_send,
    r_send,
    r_recv,
    g_send,
    g_recv,
    *weight_sems,
):
    w = Where(n_dp, n_seq)
    dp, me = w.dp, w.me
    every = n_dp * n_seq
    flat = dp * n_seq + me
    head = wk_hbm.shape[2]
    heads_wide = wq_buf.shape[3]
    rows, width = tok_ref.shape

    sources = (
        (wk_hbm, wkv_buf.at[me, :, :, pl.ds(0, head)]),
        (wv_hbm, wkv_buf.at[me, :, :, pl.ds(head, head)]),
        (wq_hbm, wq_buf.at[me]),
        (tok_hbm, tok_ref),
        (wo_hbm, wo_ref),
        (roww_hbm, roww_ref),
        (colw_hbm, colw_ref),
        (cot_hbm, cot_ref),
    )
    loads = [
        pltpu.make_async_copy(src, dst, load_sem.at[i]) for i, (src, dst) in enumerate(sources)
    ]
    for load in loads:
        load.start()

    barrier = pltpu.get_barrier_semaphore()

    def greet(t, unused):
        peer = (flat + t) % every
        pl.semaphore_signal(
            barrier, inc=1, device_id=(peer // n_seq, peer % n_seq), device_id_type=MESH
        )
        return unused

    lax.fori_loop(1, every, greet, 0)
    loads[0].wait()
    loads[1].wait()
    loads[2].wait()
    pl.semaphore_wait(barrier, every - 1)
    wkv = Gather(w, lambda s: wkv_buf.at[s], weight_sems[0], weight_sems[1])
    wq = Shared(w, wq_buf, weight_sems[2:7])
    wkv.start()
    wq.start()
    loads[3].wait()
    tok = tok_ref[...].astype(F32)
    normed = (tok * lax.rsqrt(jnp.mean(tok * tok, axis=1, keepdims=True) + 1e-06)).astype(BF16)
    wkv.pass_line()
    wkv.pass_mid()
    wkv.complete()

    def whole(buf):
        return merge_rows(buf[...].reshape(n_seq * 3, buf.shape[2], buf.shape[3]), width)

    kv_ref[me] = jnp.dot(normed, whole(wkv_buf), preferred_element_type=F32).astype(BF16)
    blocks = Gather(w, lambda s: kv_ref.at[s], k_send, k_recv)
    blocks.start()
    wq.pass_line()
    blocks.pass_line()
    wq.pass_mid()
    blocks.pass_mid()
    wq.pass_across()
    wq.complete()
    queries = jnp.dot(normed, whole(wq_buf), preferred_element_type=F32).astype(BF16)
    blocks.complete()
    length = n_seq * rows
    keys = kv_ref[:, :, 0:head].reshape(length, head)
    values = kv_ref[:, :, head : 2 * head].reshape(length, head)
    factor = math.log2(math.e) / math.sqrt(head)
    for h in range(0, heads_wide // head, 2):
        both = jnp.concatenate(
            [queries[:, h * head : (h + 1) * head], queries[:, (h + 1) * head : (h + 2) * head]],
            axis=0,
        )
        scores = lax.dot_general(both, keys, LAST, preferred_element_type=F32)
        top = jnp.max(scores, axis=1, keepdims=True)
        weights = jnp.exp2((scores - top) * factor)
        total = jnp.sum(weights, axis=1, keepdims=True)
        out = jnp.dot(weights.astype(BF16), values, preferred_element_type=F32) / total
        out = out.astype(BF16)
        att[:, h * head : (h + 1) * head] = out[0:rows]
        att[:, (h + 1) * head : (h + 2) * head] = out[rows : 2 * rows]
    bins = rows // POOL
    count = n_seq * bins
    binned[me] = jnp.sum(att[...].astype(F32).reshape(bins, POOL, heads_wide), axis=1)
    for load in loads[4:]:
        load.wait()
    attended = Gather(w, lambda s: binned.at[s], b_send, b_recv)
    attended.start()
    attended.pass_on()
    attended.complete()
    summed = binned[...].reshape(count, heads_wide)
    high = summed.astype(BF16)
    low = (summed - high.astype(F32)).astype(BF16)
    update = lax.dot_general(wo_ref[...], high, LAST, preferred_element_type=F32)
    update = update + lax.dot_general(wo_ref[...], low, LAST, preferred_element_type=F32)
    pooled_ref[me] = update * (1.0 / POOL)
    own = Gather(w, lambda s: pooled_ref.at[s], f_send, f_recv)
    own.start()
    own.pass_on()
    own.complete()
    pooled = pooled_ref[...].reshape(width, count)
    scale = lax.rsqrt(jnp.mean(pooled * pooled, axis=0, keepdims=True) + 1e-06)
    feat = (pooled * scale).astype(BF16)
    turned[dp] = feat
    share_rows = width // 2

    def piece(p, core):
        return turned.at[p, pl.ds(pl.multiple_of(core * share_rows, share_rows), share_rows)]

    def across(d):
        ref = piece(dp, w.core)
        return pltpu.make_async_remote_copy(
            src_ref=ref,
            dst_ref=ref,
            send_sem=x_send.at[d],
            recv_sem=x_recv.at[dp, w.core],
            device_id=((dp + d) % n_dp, me),
            device_id_type=MESH,
        )

    def beside(d, core):
        other = (dp + d) % n_dp
        ref = piece(other, core)
        return pltpu.make_async_remote_copy(
            src_ref=ref,
            dst_ref=ref,
            send_sem=s_send.at[d],
            recv_sem=x_recv.at[other, core],
            device_id=(dp, w.at(0, 0, True)),
            device_id_type=MESH,
        )

    def each(total, act):
        def step(k, unused):
            act(k)
            return unused

        lax.fori_loop(0, total, step, 0)

    def save(src, dst, i):
        copy = pltpu.make_async_copy(src, dst, save_sem.at[i])
        copy.start()
        return copy

    saves = [save(turned.at[dp], turned_out.at[dp], 0)]
    feat_rows = feat.T
    row_all = jnp.dot(feat_rows, roww_ref[...], preferred_element_type=F32).astype(BF16)
    col_proj = jnp.dot(feat_rows, colw_ref[...], preferred_element_type=F32).astype(BF16)
    rowp_ref[...] = row_all.astype(F32).reshape(rowp_ref.shape)
    col_wide = col_proj.astype(F32)
    colp_ref[...] = col_wide
    saves.append(save(rowp_ref.at[me], rowp_out, 1))
    saves.append(save(colp_ref, colp_out, 2))
    row_wide = rowp_ref[me]
    sums = jnp.zeros(col_wide.shape, F32)
    for i in range(bins):
        sums = sums + cot_ref[i].astype(F32) * row_wide[i : i + 1, :]
    terms[...] = sums.reshape(terms.shape)

    def scatter(t):
        peer = (me + t) % n_seq
        return pltpu.make_async_remote_copy(
            src_ref=terms.at[peer],
            dst_ref=parts.at[me],
            send_sem=r_send.at[t],
            recv_sem=r_recv.at[me],
            device_id=(dp, peer),
            device_id_type=MESH,
        )

    def scattered(t):
        peer = (me + t) % n_seq
        return pltpu.make_async_remote_copy(
            src_ref=terms.at[me],
            dst_ref=parts.at[peer],
            send_sem=r_send.at[t],
            recv_sem=r_recv.at[peer],
            device_id=(dp, peer),
            device_id_type=MESH,
        )

    each(n_seq - 1, lambda k: scatter(k + 1).start())
    for d in range(1, n_dp):
        across(d).start()

    parts[me] = terms[me]
    row_list = []
    for i in range(bins):
        row_list.append(jnp.sum(cot_ref[i].astype(F32) * col_wide, axis=0, keepdims=True))
    row_grad = jnp.concatenate(row_list, axis=0)
    each(n_seq - 1, lambda k: scattered(k + 1).wait_recv())
    col_grad = jnp.sum(parts[...], axis=0)
    grads[flat] = jnp.concatenate([row_grad, col_grad], axis=1).astype(BF16)

    def share(t):
        peer = (flat + t) % every
        return pltpu.make_async_remote_copy(
            src_ref=grads.at[flat],
            dst_ref=grads.at[flat],
            send_sem=g_send.at[t],
            recv_sem=g_recv.at[flat],
            device_id=(peer // n_seq, peer % n_seq),
            device_id_type=MESH,
        )

    def shared(t):
        peer = (flat + t) % every
        return pltpu.make_async_remote_copy(
            src_ref=grads.at[peer],
            dst_ref=grads.at[peer],
            send_sem=g_send.at[t],
            recv_sem=g_recv.at[peer],
            device_id=(dp, me),
            device_id_type=MESH,
        )

    each(every - 1, lambda k: share(k + 1).start())

    for d in range(1, n_dp):
        beside(d, w.core).wait_recv()
        beside(d, w.core).start()
    for d in range(1, n_dp):
        beside(d, 1 - w.core).wait_recv()
        other = (dp + d) % n_dp
        saves.append(save(turned.at[other], turned_out.at[other], 3 + d))
    each(every - 1, lambda k: shared(k + 1).wait_recv())
    saves.append(save(grads, grads_out, 3))
    for weights in (wkv, wq, blocks, attended, own):
        weights.drain()
    for d in range(1, n_dp):
        across(d).wait_send()
        beside(d, w.core).wait_send()
    each(n_seq - 1, lambda k: scatter(k + 1).wait_send())
    each(every - 1, lambda k: share(k + 1).wait_send())
    for copy in saves:
        copy.wait()


def tail_kernel(rowp_ref, colp_ref, turned, grads, pair_ref, grow_ref, gcol_ref):
    for i in range(rowp_ref.shape[0]):
        pair_ref[i] = (rowp_ref[i : i + 1, :] * colp_ref[...]).astype(BF16)
    n_dp, width, count = turned.shape
    whole = merge_rows(grads[...], n_dp * count)
    total = jnp.zeros((width, whole.shape[1]), F32)
    for p in range(n_dp):
        part = whole[p * count : (p + 1) * count]
        total = total + jnp.dot(turned[p], part, preferred_element_type=F32)
    total = total.astype(BF16)
    channels = grow_ref.shape[1]
    grow_ref[...] = total[:, 0:channels]
    gcol_ref[...] = total[:, channels : 2 * channels]


def on_device(
    n_dp,
    n_seq,
    tokens,
    query_weight,
    key_weight,
    value_weight,
    output_weight,
    row_weight,
    col_weight,
    pair_cotangent,
):
    rows, width = tokens.shape[1:]
    head = key_weight.shape[1]
    heads_wide = query_weight.shape[1]
    bins, count, channels = pair_cotangent.shape[1:]
    third = key_weight.shape[0] // 3
    vmem = pl.BlockSpec(memory_space=pltpu.VMEM)
    hbm = pl.BlockSpec(memory_space=pltpu.HBM)
    dma = pltpu.SemaphoreType.DMA
    moves = copies_of(n_seq)
    every = n_dp * n_seq
    grant = 60 * 2**20
    kept = pl.pallas_call(
        functools.partial(main_kernel, n_dp, n_seq),
        out_shape=(
            jax.ShapeDtypeStruct((bins, channels), F32),
            jax.ShapeDtypeStruct((count, channels), F32),
            jax.ShapeDtypeStruct((n_dp, width, count), BF16),
            jax.ShapeDtypeStruct((every, bins, 2 * channels), BF16),
        ),
        in_specs=[hbm] * 8,
        out_specs=(hbm,) * 4,
        scratch_shapes=[
            pltpu.VMEM((n_seq, bins, channels), F32),
            pltpu.VMEM((count, channels), F32),
            pltpu.VMEM((n_dp, width, count), BF16),
            pltpu.VMEM((every, bins, 2 * channels), BF16),
            pltpu.VMEM((rows, width), BF16),
            pltpu.VMEM((width, channels), BF16),
            pltpu.VMEM((width, channels), BF16),
            pltpu.VMEM((bins, count, channels), BF16),
            pltpu.VMEM((n_seq, 3, third, 2 * head), BF16),
            pltpu.VMEM((n_seq, 3, third, heads_wide), BF16),
            pltpu.VMEM(output_weight.shape, BF16),
            pltpu.VMEM((n_seq, rows, 2 * head), BF16),
            pltpu.VMEM((rows, heads_wide), BF16),
            pltpu.VMEM((n_seq, bins, heads_wide), F32),
            pltpu.VMEM((n_seq, 3 * third, count), F32),
            pltpu.VMEM((n_seq, bins, channels), F32),
            pltpu.VMEM((n_seq, bins, channels), F32),
            dma((8,)),
            dma((3 + n_dp,)),
            *[dma((moves,)), dma((n_seq,))] * 3,
            dma((n_dp,)),
            dma((n_dp, 2)),
            dma((n_dp,)),
            dma((n_seq,)),
            dma((n_seq,)),
            dma((every,)),
            dma((every,)),
            *shared_sems(n_seq)[:2],
            *shared_sems(n_seq),
        ],
        compiler_params=pltpu.CompilerParams(
            collective_id=0, has_side_effects=True, vmem_limit_bytes=grant
        ),
    )(
        tokens[0],
        query_weight.reshape(3, third, heads_wide),
        key_weight.reshape(3, third, head),
        value_weight.reshape(3, third, head),
        output_weight,
        row_weight,
        col_weight,
        pair_cotangent[0],
    )
    pair, grow, gcol = pl.pallas_call(
        tail_kernel,
        out_shape=(
            jax.ShapeDtypeStruct((bins, count, channels), BF16),
            jax.ShapeDtypeStruct((width, channels), BF16),
            jax.ShapeDtypeStruct((width, channels), BF16),
        ),
        in_specs=[vmem] * 4,
        out_specs=(vmem,) * 3,
        compiler_params=pltpu.CompilerParams(vmem_limit_bytes=grant),
    )(*kept)
    return (pair[None], grow, gcol)


def solution(mesh):
    placed = (
        P("dp", "seq", None),
        P("seq", None),
        P("seq", None),
        P("seq", None),
        P("seq", None),
        P(),
        P(),
        P("dp", "seq", None, None),
    )
    return jax.shard_map(
        functools.partial(on_device, mesh.shape["dp"], mesh.shape["seq"]),
        mesh=mesh,
        in_specs=placed,
        out_specs=(P("dp", "seq", None, None), P(), P()),
        check_vma=False,
    )
```
